32 devices in a mesh: groups: 2 (over x), seq: 16 (over z, y, core).
Axes of the slice: x: 2, y: 2, z: 4, core: 2. Of those that a mesh axis runs over, the one named last changes fastest.
Arguments:
- queries: bfloat16 [8192, 2048], P(('groups', 'seq')), parts along dimension 0, may hold values from -9 to 9
- keys: bfloat16 [8192, 512], P(('groups', 'seq')), parts along dimension 0, may hold values from -9 to 9
- values: bfloat16 [8192, 512], P(('groups', 'seq')), parts along dimension 0, may hold values from -6 to 6
- segment: int32 [8192], P(('groups', 'seq')), parts along dimension 0, may hold values from 0 to 10, never falling along the last dimension, each value on 1 to 769 neighbouring positions
- out_weight: bfloat16 [2048, 4096], P('seq'), may hold values from -0.125 to 0.125
Outputs:
- projected: bfloat16 [8192, 4096], P(('groups', 'seq')), parts along dimension 0
The draws below stay inside these ranges and needn't reach their ends.
There are 2 independent parts, one for each index of `groups`. The reference program is written for one: setup_inputs(seed, part) draws one part's arguments, and reference() takes and returns one part's arrays. A program takes and returns all parts, laid end to end along the dimension named above; an argument that names none is the same for every part. Nothing has to cross between parts.
Inputs may be any that keep to these rules, and one draw needn't show every extreme that they name: `segment`: document numbers never fall along the stretch; every document has 1 to 769 tokens.
All inputs are finite; a program needn't handle non-finite values.
Results may differ from the reference program's by a relative error of at most 0.0053.
Values may be sent and summed in bfloat16 or wider, within the bound.
No kernel may reach another device: no remote copies, remote signals or barrier semaphores. Data moves between devices by JAX's collectives and lax.ppermute only.
A program may use at most 128 MiB of HBM per device.

```python
import math
import jax
import jax.numpy as jnp
import numpy as np
from jax import lax

D = 4096
HEADS = 16
KV_HEADS = 4
HEAD = 128
TOK_DEV = 256
SPAN = 4
MOST = 769
TOKENS = 4096
DOCS = 11
N_SEQ = 16


def draw_queries(key, part):
    shape_four = (TOKENS, KV_HEADS, HEADS // KV_HEADS, HEAD)
    base_draw = jnp.clip(jax.random.normal(jax.random.fold_in(key, 1), shape_four, jnp.float32), -4.0, 4.0)
    return base_draw.reshape(TOKENS, HEADS * HEAD).astype(jnp.bfloat16)


def draw_keys(key, part):
    shape_three = (TOKENS, KV_HEADS, HEAD)
    base_draw = jnp.clip(jax.random.normal(jax.random.fold_in(key, 2), shape_three, jnp.float32), -4.0, 4.0)
    return base_draw.reshape(TOKENS, KV_HEADS * HEAD).astype(jnp.bfloat16)


def block_scale(key, extent, cuts, low, high):
    gain, own = 1.0, jax.random.fold_in(key, 6)
    for position, shards_of in cuts:
        heights = jnp.exp(jax.random.uniform(jax.random.fold_in(own, position), (shards_of,), jnp.float32, low / len(cuts), high / len(cuts)))
        gain = gain * jnp.repeat(heights, extent[position] // shards_of).reshape([-1 if axis == position else 1 for axis in range(len(extent))])
    return gain


def split_up(number_of, total, bound, slope):
    weights = [(1 << 20) // math.isqrt(rank ** slope) + 1 for rank in range(2, number_of + 1)]
    surplus, holding = total - bound - (number_of - 1), [1] * (number_of - 1)
    while surplus > 0:
        free = [i for i in range(number_of - 1) if holding[i] < bound]
        whole, remaining = sum([weights[i] for i in free]), surplus
        for i in free:
            addition = min(bound - holding[i], max(1, remaining * weights[i] // whole), surplus)
            holding[i] = holding[i] + addition
            surplus = surplus - addition
    return np.array([bound] + holding)


def ragged(key, amount, total, most, lean):
    if amount == 2:
        one = jax.random.randint(key, (), max(1, total - most), min(most, total - 1) + 1)
        return jnp.stack([one, total - one])
    sizes = jnp.asarray(split_up(amount, total, most, lean), jnp.int32)
    couples = (amount - 1) // 2
    donor, taker = sizes[1:1 + 2 * couples:2], sizes[2:2 + 2 * couples:2]
    room = jnp.minimum(donor - 1, most - taker)
    moved = jax.random.randint(jax.random.fold_in(key, 1), (couples,), 0, 1 << 20) % (room + 1)
    sizes = sizes.at[1:1 + 2 * couples:2].set(donor - moved).at[2:2 + 2 * couples:2].set(taker + moved)
    return sizes[jax.random.permutation(jax.random.fold_in(key, 2), amount)]


def gaussian(own_key, shape, width, most, pieces=(), kind=jnp.bfloat16):
    gain = block_scale(own_key, shape, pieces, -0.22, 0.18) if pieces else 1.0
    values = jax.random.normal(own_key, shape, jnp.float32) * width * gain
    return jnp.minimum(jnp.maximum(values, -most), most).astype(kind)


def setup_inputs(seed: int = 0, part: int = 0) -> dict:
    key_list = jax.random.split(jax.random.key(seed), 6)
    part_splits = jax.random.split(jax.random.fold_in(key_list[5], part), 6)
    queries = draw_queries(jax.random.fold_in(jax.random.fold_in(key_list[5], part), 71), part)
    keys = draw_keys(jax.random.fold_in(jax.random.fold_in(key_list[5], part), 71), part)
    values = gaussian(part_splits[2], (TOKENS, KV_HEADS * HEAD), 1.0, 6.0, ((0, 16),))
    segment = jnp.searchsorted(jnp.cumsum(ragged(part_splits[3], DOCS, TOKENS, MOST, 1)), jnp.arange(TOKENS), side="right").astype(jnp.int32)
    out_weight = gaussian(key_list[4], (HEADS * HEAD, D), (HEADS * HEAD) ** -0.5, 0.125, ((0, 16),))
    return dict(queries=queries, keys=keys, values=values, segment=segment, out_weight=out_weight)


def one_head(query_group, key_head, value_head, live_mask):
    scores = jnp.einsum("thd,sd->ths", query_group.astype(jnp.float32), key_head.astype(jnp.float32)) * (HEAD ** -0.5)
    scores = jnp.where(live_mask[:, None, :], scores, -jnp.inf)
    row_max = jnp.max(scores, axis=-1, keepdims=True)
    weights = jnp.exp(scores - row_max)
    weight_sum = jnp.sum(weights, axis=-1, keepdims=True)
    probabilities = weights.astype(jnp.bfloat16)
    head_mix = jnp.einsum("ths,sd->thd", probabilities.astype(jnp.float32), value_head.astype(jnp.float32))
    return head_mix / weight_sum


def attend(queries_block, keys_window, values_window, live_mask):
    row_count = queries_block.shape[0]
    window_rows = keys_window.shape[0]
    group_size = HEADS // KV_HEADS
    query_heads = queries_block.reshape(row_count, KV_HEADS, group_size, HEAD).transpose(1, 0, 2, 3)
    key_heads = keys_window.reshape(window_rows, KV_HEADS, HEAD).transpose(1, 0, 2)
    value_heads = values_window.reshape(window_rows, KV_HEADS, HEAD).transpose(1, 0, 2)

    def per_group(operands):
        return one_head(operands[0], operands[1], operands[2], live_mask)

    head_outputs = lax.map(per_group, (query_heads, key_heads, value_heads))
    return head_outputs.transpose(1, 0, 2, 3).reshape(row_count, HEADS * HEAD).astype(jnp.bfloat16)


def reference(queries, keys, values, segment, out_weight):
    pad_rows = (SPAN - 1) * TOK_DEV
    keys_padded = jnp.concatenate([jnp.zeros((pad_rows, keys.shape[1]), keys.dtype), keys], axis=0)
    values_padded = jnp.concatenate([jnp.zeros((pad_rows, values.shape[1]), values.dtype), values], axis=0)
    segment_padded = jnp.concatenate([jnp.full((pad_rows,), -1, jnp.int32), segment.astype(jnp.int32)], axis=0)

    def per_block(block_id):
        first_row = (block_id * TOK_DEV).astype(jnp.int32)
        queries_block = lax.dynamic_slice_in_dim(queries, first_row, TOK_DEV, 0)
        keys_window = lax.dynamic_slice_in_dim(keys_padded, first_row, SPAN * TOK_DEV, 0)
        values_window = lax.dynamic_slice_in_dim(values_padded, first_row, SPAN * TOK_DEV, 0)
        segment_query = lax.dynamic_slice_in_dim(segment.astype(jnp.int32), first_row, TOK_DEV, 0)
        segment_key = lax.dynamic_slice_in_dim(segment_padded, first_row, SPAN * TOK_DEV, 0)
        query_pos = first_row + jnp.arange(TOK_DEV, dtype=jnp.int32)
        key_pos = first_row - pad_rows + jnp.arange(SPAN * TOK_DEV, dtype=jnp.int32)
        live_mask = (segment_query[:, None] == segment_key[None, :]) & (key_pos[None, :] <= query_pos[:, None])
        attention = attend(queries_block, keys_window, values_window, live_mask)
        return jnp.dot(attention, out_weight, preferred_element_type=jnp.float32).astype(jnp.bfloat16)

    blocks = lax.map(per_block, jnp.arange(N_SEQ, dtype=jnp.int32))
    return blocks.reshape(TOKENS, out_weight.shape[1])
```

```python
import functools
import math

import jax
import jax.numpy as jnp
from jax import lax
from jax.experimental import pallas as pl
from jax.experimental.pallas import tpu as pltpu
from jax.sharding import PartitionSpec as P


HEADS = 16
KV_HEADS = 4
HEAD = 128
SPAN = 4
GROUP = HEADS // KV_HEADS
EXTRA = 16
CHUNKS = 2
ATT_PARTS = 2
BELOW = -1e30
AXES = ("groups", "seq")


def moved(value, groups, seq, move):
    route = []
    for g in range(groups):
        for s in range(seq):
            to = move(g, s)
            if to is not None:
                route.append((g * seq + s, to[0] * seq + to[1]))
    return lax.ppermute(value, AXES, route)


def attention_kernel(q_ref, sq_ref, *refs):
    count = SPAN
    k_refs, v_refs, s_refs = refs[:count], refs[count : 2 * count], refs[2 * count : 3 * count]
    o_ref, bias_ref = refs[3 * count], refs[3 * count + 1]
    rows = q_ref.shape[0]
    me = lax.axis_index("seq")
    odd = lax.rem(me, 2)
    sources = (me, me - 2, me - 3 + 2 * odd, me - 1 - 2 * odd)

    @pl.when(pl.program_id(0) == 0)
    def _():
        own = sq_ref[:, 0:1].astype(jnp.float32)
        for block in range(count):
            there = s_refs[block][0:1, :].astype(jnp.float32)
            there = jnp.where(sources[block] >= 0, there, -1.0)
            live = own == there
            if block == 0:
                at_row = lax.broadcasted_iota(jnp.int32, (rows, rows), 0)
                at_column = lax.broadcasted_iota(jnp.int32, (rows, rows), 1)
                live = live & (at_column <= at_row)
            bias_ref[:, block * rows : (block + 1) * rows] = jnp.where(live, 0.0, BELOW)

    scale = HEAD ** (-0.5) * math.log2(math.e)
    for head in range(GROUP):
        q = q_ref[:, head * HEAD : (head + 1) * HEAD]
        scores = []
        for block in range(count):
            s = lax.dot_general(
                q, k_refs[block][0:rows, :], (((1,), (1,)), ((), ())),
                preferred_element_type=jnp.float32,
            )
            scores.append(s + bias_ref[:, block * rows : (block + 1) * rows])
        top = functools.reduce(jnp.maximum, scores)
        top = jnp.max(top, axis=1, keepdims=True)
        total = None
        mixed = None
        for block in range(count):
            weights = jnp.exp2((scores[block] - top) * scale)
            total = weights if total is None else total + weights
            part = jnp.dot(
                weights.astype(jnp.bfloat16), v_refs[block][0:rows, :],
                preferred_element_type=jnp.float32,
            )
            mixed = part if mixed is None else mixed + part
        total = jnp.sum(total, axis=1, keepdims=True)
        o_ref[:, head * HEAD : (head + 1) * HEAD] = (mixed / total).astype(o_ref.dtype)


def attend(queries, own_segment, windows, first, parts):
    rows = queries.shape[0]
    width = GROUP * HEAD
    groups = KV_HEADS // parts
    base = first * groups
    rows_in = windows[0].shape[0]
    k_spec = pl.BlockSpec((rows_in, HEAD), lambda i: (0, base + i))
    v_spec = pl.BlockSpec((rows_in, HEAD), lambda i: (0, KV_HEADS + base + i))
    s_spec = pl.BlockSpec((EXTRA, rows), lambda i: (rows // EXTRA, 0))
    flops = 4 * rows * SPAN * rows * HEAD * GROUP * groups
    return pl.pallas_call(
        attention_kernel,
        grid=(groups,),
        in_specs=[
            pl.BlockSpec((rows, width), lambda i: (0, base + i)),
            pl.BlockSpec((rows, HEAD), lambda i: (0, 0)),
        ]
        + [k_spec] * SPAN
        + [v_spec] * SPAN
        + [s_spec] * SPAN,
        out_specs=pl.BlockSpec((rows, width), lambda i: (0, i)),
        out_shape=jax.ShapeDtypeStruct((rows, groups * width), jnp.bfloat16),
        scratch_shapes=[pltpu.VMEM((rows, SPAN * rows), jnp.float32)],
        cost_estimate=pl.CostEstimate(
            flops=flops, bytes_accessed=4 * rows * groups * width, transcendentals=rows * rows * SPAN * GROUP * groups
        ),
    )(queries, own_segment, *windows, *windows, *windows)


def project_kernel(seq, layout, depth, count, *refs):
    parts = refs[:count]
    piece_refs = refs[count : count + len(layout)]
    o_ref, held, sem = refs[count + len(layout) :]
    me = lax.axis_index("seq")
    for which, (flip, start, shifts) in enumerate(layout):
        near = lax.bitwise_xor(me, flip)
        for at, shift in enumerate(shifts):
            source = lax.rem(near - 4 * shift + seq, seq)
            rows = pl.ds(pl.multiple_of(source * depth, depth), depth)
            pltpu.make_async_copy(
                piece_refs[which].at[(start + at) * depth : (start + at + 1) * depth, :],
                held.at[rows, :],
                sem.at[which],
            ).start()
    for which, (flip, start, shifts) in enumerate(layout):
        size = len(shifts) * depth
        piece = piece_refs[which].at[start * depth : start * depth + size, :]
        pltpu.make_async_copy(piece, held.at[0:size, :], sem.at[which]).wait()
    width = o_ref.shape[1]
    tile = min(256, width)
    for left in range(0, width, tile):
        total = None
        for at, part in enumerate(parts):
            span = part.shape[1]
            product = jnp.dot(
                part[...], held[at * span : (at + 1) * span, left : left + tile],
                preferred_element_type=jnp.float32,
            )
            total = product if total is None else total + product
        o_ref[:, left : left + tile] = total.astype(o_ref.dtype)


def project(parts, pieces, layout, seq, depth):
    rows = parts[0].shape[0]
    width = pieces[0].shape[1]
    inner = seq * depth
    return pl.pallas_call(
        functools.partial(project_kernel, seq, layout, depth, len(parts)),
        in_specs=[pl.BlockSpec(memory_space=pltpu.VMEM)] * len(parts)
        + [pl.BlockSpec(memory_space=pl.ANY)] * len(pieces),
        out_specs=pl.BlockSpec(memory_space=pltpu.VMEM),
        out_shape=jax.ShapeDtypeStruct((rows, width), jnp.bfloat16),
        scratch_shapes=[
            pltpu.VMEM((inner, width), jnp.bfloat16),
            pltpu.SemaphoreType.DMA((len(pieces),)),
        ],
        cost_estimate=pl.CostEstimate(
            flops=2 * rows * inner * width, bytes_accessed=2 * inner * width, transcendentals=0
        ),
    )(*parts, *pieces)


def body(groups, seq, queries, keys, values, segment, out_weight):
    rows = queries.shape[0]
    depth, columns = out_weight.shape
    share = columns // groups
    width = share // CHUNKS
    group = lax.axis_index("groups")
    go = lambda value, move: moved(value, groups, seq, move)

    def at(s):
        return s if 0 <= s < seq else None

    def seq_move(step):
        def move(g, s):
            to = at(step(s))
            return None if to is None else (g, to)

        return move

    shifts = line_shifts(seq)

    marks = jnp.pad(
        segment.astype(jnp.bfloat16)[None, :],
        ((0, EXTRA - 1), (0, 2 * KV_HEADS * HEAD - rows)),
    )
    packed = jnp.concatenate(
        [jnp.concatenate([keys, values], axis=1), marks], axis=0
    )
    own_segment = jnp.broadcast_to(
        segment.astype(jnp.bfloat16)[:, None], (rows, HEAD)
    )
    back2 = go(packed, seq_move(lambda s: s + 2))
    back_odd = go(packed, seq_move(lambda s: s + 1 if s % 2 == 0 else s + 3))
    mine = lax.dynamic_slice(out_weight, (0, group * share), (depth, share))
    mine = jnp.concatenate([mine[:, c * width : (c + 1) * width] for c in range(CHUNKS)], axis=0)
    mine_across = go(mine, seq_move(lambda s: s ^ 2))

    def cut(value, chunk):
        return value[chunk * depth : (chunk + 1) * depth]

    held = [[] for _ in range(CHUNKS)]
    for chunk in range(CHUNKS):
        for shift in shifts:
            held[chunk].append(go(cut(mine, chunk), seq_move(lambda s, k=shift: (s + 4 * k) % seq)))
    back_swap = go(back2, seq_move(lambda s: s ^ 1))
    mine_swap = go(mine, seq_move(lambda s: s ^ 1))
    mine_across_swap = go(mine_across, seq_move(lambda s: s ^ 1))
    windows = (packed, back2, back_odd, back_swap)
    att, att_far = [], []
    for part in range(ATT_PARTS):
        att.append(attend(queries, own_segment, windows, part, ATT_PARTS))
        att_far.append(go(att[part], lambda g, s: ((g + 1) % groups, s)))
    near_out, far_out = [], []
    for chunk in range(CHUNKS):
        line = jnp.concatenate(held[chunk], axis=0)
        across = go(line, seq_move(lambda s: s ^ 2))
        line_swap = go(line, seq_move(lambda s: s ^ 1))
        across_swap = go(across, seq_move(lambda s: s ^ 1))
        layout = tuple((flip, chunk, (0,)) for flip in range(4))
        layout = layout + tuple((flip, 0, tuple(shifts)) for flip in range(4))
        pieces = [mine, mine_swap, mine_across, mine_across_swap]
        pieces += [line, line_swap, across, across_swap]
        far = project(att_far, pieces, layout, seq, depth)
        far_out.append(go(far, lambda g, s: ((g + 1) % groups, s)))
        near_out.append(project(att, pieces, layout, seq, depth))
    near_first = group == 0
    first = [jnp.where(near_first, a, b) for a, b in zip(near_out, far_out)]
    second = [jnp.where(near_first, b, a) for a, b in zip(near_out, far_out)]
    return jnp.concatenate(first + second, axis=1)


def line_shifts(seq):
    return [1, seq // 4 - 1] + list(range(2, seq // 4 - 1))


def solution(mesh):
    in_specs = (
        P(("groups", "seq"), None),
        P(("groups", "seq"), None),
        P(("groups", "seq"), None),
        P(("groups", "seq")),
        P("seq", None),
    )
    out_specs = P(("groups", "seq"), None)
    local = functools.partial(body, mesh.shape["groups"], mesh.shape["seq"])
    return jax.shard_map(local, mesh=mesh, in_specs=in_specs, out_specs=out_specs, check_vma=False)
```

```python
import functools
import math

import jax
import jax.numpy as jnp
from jax import lax
from jax.experimental import pallas as pl
from jax.experimental.pallas import tpu as pltpu
from jax.sharding import PartitionSpec as P


HEADS = 16
KV_HEADS = 4
HEAD = 128
SPAN = 4
GROUP = HEADS // KV_HEADS
EXTRA = 16
CHUNKS = 2
ATT_PARTS = 2
BELOW = -1e30
SMALL = 24 << 20
AXES = ("groups", "seq")


def moved(value, groups, seq, move):
    route = []
    for g in range(groups):
        for s in range(seq):
            to = move(g, s)
            if to is not None:
                route.append((g * seq + s, to[0] * seq + to[1]))
    return lax.ppermute(value, AXES, route)


def attention_kernel(q_ref, sq_ref, *refs):
    count = SPAN
    k_refs, v_refs, s_refs = refs[:count], refs[count : 2 * count], refs[2 * count : 3 * count]
    o_ref, bias_ref = refs[3 * count], refs[3 * count + 1]
    rows = q_ref.shape[0]
    me = lax.axis_index("seq")
    odd = lax.rem(me, 2)
    sources = (me, me - 2, me - 3 + 2 * odd, me - 1 - 2 * odd)

    @pl.when(pl.program_id(0) == 0)
    def _():
        own = sq_ref[:, 0:1].astype(jnp.float32)
        for block in range(count):
            there = s_refs[block][0:1, :].astype(jnp.float32)
            there = jnp.where(sources[block] >= 0, there, -1.0)
            live = own == there
            if block == 0:
                at_row = lax.broadcasted_iota(jnp.int32, (rows, rows), 0)
                at_column = lax.broadcasted_iota(jnp.int32, (rows, rows), 1)
                live = live & (at_column <= at_row)
            bias_ref[:, block * rows : (block + 1) * rows] = jnp.where(live, 0.0, BELOW)

    scale = HEAD ** (-0.5) * math.log2(math.e)
    for head in range(GROUP):
        q = q_ref[:, head * HEAD : (head + 1) * HEAD]
        scores = []
        for block in range(count):
            s = lax.dot_general(
                q, k_refs[block][0:rows, :], (((1,), (1,)), ((), ())),
                preferred_element_type=jnp.float32,
            )
            scores.append(s + bias_ref[:, block * rows : (block + 1) * rows])
        top = functools.reduce(jnp.maximum, scores)
        top = jnp.max(top, axis=1, keepdims=True)
        total = None
        mixed = None
        for block in range(count):
            weights = jnp.exp2((scores[block] - top) * scale)
            total = weights if total is None else total + weights
            part = jnp.dot(
                weights.astype(jnp.bfloat16), v_refs[block][0:rows, :],
                preferred_element_type=jnp.float32,
            )
            mixed = part if mixed is None else mixed + part
        total = jnp.sum(total, axis=1, keepdims=True)
        o_ref[:, head * HEAD : (head + 1) * HEAD] = (mixed / total).astype(o_ref.dtype)


def attend(queries, own_segment, windows, first, parts):
    rows = queries.shape[0]
    width = GROUP * HEAD
    groups = KV_HEADS // parts
    base = first * groups
    rows_in = windows[0].shape[0]
    k_spec = pl.BlockSpec((rows_in, HEAD), lambda i: (0, base + i))
    v_spec = pl.BlockSpec((rows_in, HEAD), lambda i: (0, KV_HEADS + base + i))
    s_spec = pl.BlockSpec((EXTRA, rows), lambda i: (rows // EXTRA, 0))
    flops = 4 * rows * SPAN * rows * HEAD * GROUP * groups
    return pl.pallas_call(
        attention_kernel,
        grid=(groups,),
        in_specs=[
            pl.BlockSpec((rows, width), lambda i: (0, base + i)),
            pl.BlockSpec((rows, HEAD), lambda i: (0, 0)),
        ]
        + [k_spec] * SPAN
        + [v_spec] * SPAN
        + [s_spec] * SPAN,
        out_specs=pl.BlockSpec((rows, width), lambda i: (0, i)),
        out_shape=jax.ShapeDtypeStruct((rows, groups * width), jnp.bfloat16),
        scratch_shapes=[pltpu.VMEM((rows, SPAN * rows), jnp.float32)],
        cost_estimate=pl.CostEstimate(
            flops=flops, bytes_accessed=4 * rows * groups * width, transcendentals=rows * rows * SPAN * GROUP * groups
        ),
        compiler_params=pltpu.CompilerParams(vmem_limit_bytes=SMALL),
    )(queries, own_segment, *windows, *windows, *windows)


def prep_kernel(cores, k_ref, v_ref, seg_ref, w_ref, packed_ref, col_ref, own_ref, give_ref, sem):
    rows, kept = k_ref.shape
    width = own_ref.shape[1]
    core = lax.rem(lax.axis_index("seq"), cores)
    base = lax.axis_index("groups") * cores
    mine = pl.ds(pl.multiple_of((base + core) * width, width), width)
    other = pl.ds(pl.multiple_of((base + cores - 1 - core) * width, width), width)
    copies = [
        pltpu.make_async_copy(w_ref.at[:, other], give_ref, sem.at[0]),
        pltpu.make_async_copy(k_ref, packed_ref.at[0:rows, 0:kept], sem.at[1]),
        pltpu.make_async_copy(v_ref, packed_ref.at[0:rows, kept : 2 * kept], sem.at[2]),
        pltpu.make_async_copy(w_ref.at[:, mine], own_ref, sem.at[3]),
    ]
    for copy in copies:
        copy.start()
    marks = seg_ref[...].astype(jnp.float32)
    column = jnp.transpose(jnp.broadcast_to(marks, (HEAD, rows)))
    col_ref[...] = column.astype(col_ref.dtype)
    packed_ref[rows:, :] = jnp.zeros((EXTRA, 2 * kept), packed_ref.dtype)
    packed_ref[rows:, 0:rows] = jnp.broadcast_to(marks, (EXTRA, rows)).astype(packed_ref.dtype)
    for copy in copies:
        copy.wait()


def prepare(keys, values, segment, out_weight, cores, width):
    rows, kept = keys.shape
    depth = out_weight.shape[0]
    in_hbm = pl.BlockSpec(memory_space=pl.ANY)
    in_vmem = pl.BlockSpec(memory_space=pltpu.VMEM)
    kind = keys.dtype
    return pl.pallas_call(
        functools.partial(prep_kernel, cores),
        in_specs=[in_hbm, in_hbm, in_vmem, in_hbm],
        out_specs=[in_vmem] * 4,
        out_shape=[
            jax.ShapeDtypeStruct((rows + EXTRA, 2 * kept), kind),
            jax.ShapeDtypeStruct((rows, HEAD), kind),
            jax.ShapeDtypeStruct((depth, width), kind),
            jax.ShapeDtypeStruct((depth, width), kind),
        ],
        scratch_shapes=[pltpu.SemaphoreType.DMA((4,))],
        compiler_params=pltpu.CompilerParams(vmem_limit_bytes=SMALL),
    )(keys, values, segment[None, :], out_weight)


def pair_kernel(a_ref, b_ref, o_ref):
    depth = a_ref.shape[0]
    o_ref[0:depth, :] = a_ref[...]
    o_ref[depth:, :] = b_ref[...]


def paired(own, got):
    in_vmem = pl.BlockSpec(memory_space=pltpu.VMEM)
    shape = jax.ShapeDtypeStruct((2 * own.shape[0], own.shape[1]), own.dtype)
    return pl.pallas_call(
        pair_kernel, in_specs=[in_vmem] * 2, out_specs=in_vmem, out_shape=shape,
        compiler_params=pltpu.CompilerParams(vmem_limit_bytes=SMALL),
    )(own, got)


def project_kernel(seq, layout, depth, parts, *refs):
    att_refs = refs[: 2 * parts]
    piece_refs = refs[2 * parts : 2 * parts + len(layout)]
    o_refs = refs[2 * parts + len(layout) : 2 * parts + len(layout) + 2]
    held, sem = refs[2 * parts + len(layout) + 2 :]
    width = o_refs[0].shape[1]
    me = lax.axis_index("seq")
    core = lax.rem(me, 2)
    chips = seq // 2
    for piece, (flip, shift, left) in zip(piece_refs, layout):
        chip = lax.rem(lax.bitwise_xor(me // 2, flip) - 2 * shift + chips, chips)
        for half in range(2):
            source = chip * 2 + (core if half == 0 else 1 - core)
            rows = pl.ds(pl.multiple_of(source * depth, depth), depth)
            pltpu.make_async_copy(
                piece.at[half * depth : (half + 1) * depth, left : left + width],
                held.at[rows, :],
                sem,
            ).start()
    pltpu.make_async_copy(held, held, sem).wait()
    tile = min(256, width)
    span = att_refs[0].shape[1]
    for left in range(0, width, tile):
        for which in range(2):
            total = None
            for part in range(parts):
                product = jnp.dot(
                    att_refs[which * parts + part][...],
                    held[part * span : (part + 1) * span, left : left + tile],
                    preferred_element_type=jnp.float32,
                )
                total = product if total is None else total + product
            o_refs[which][:, left : left + tile] = total.astype(o_refs[which].dtype)


def project(first, second, pieces, layout, seq, depth, width):
    parts = len(first)
    rows = first[0].shape[0]
    inner = seq * depth
    in_vmem = pl.BlockSpec(memory_space=pltpu.VMEM)
    shape = jax.ShapeDtypeStruct((rows, width), jnp.bfloat16)
    return pl.pallas_call(
        functools.partial(project_kernel, seq, layout, depth, parts),
        in_specs=[in_vmem] * (2 * parts) + [pl.BlockSpec(memory_space=pl.ANY)] * len(pieces),
        out_specs=[in_vmem] * 2,
        out_shape=[shape, shape],
        scratch_shapes=[pltpu.VMEM((inner, width), jnp.bfloat16), pltpu.SemaphoreType.DMA],
        cost_estimate=pl.CostEstimate(
            flops=4 * rows * inner * width, bytes_accessed=2 * inner * width, transcendentals=0
        ),
        compiler_params=pltpu.CompilerParams(vmem_limit_bytes=SMALL),
    )(*first, *second, *pieces)


def join_kernel(cores, chunks, *refs):
    o_ref, sem = refs[-2:]
    width = refs[0].shape[1]
    core = lax.rem(lax.axis_index("seq"), cores)
    group = lax.axis_index("groups")
    copies = []
    for at, ref in enumerate(refs[:-2]):
        quarter, chunk = at // chunks, at % chunks
        from_group = group if quarter < 2 else 1 - group
        from_core = core if quarter % 2 == 0 else 1 - core
        left = ((from_group * cores + from_core) * chunks + chunk) * width
        copies.append(
            pltpu.make_async_copy(
                ref, o_ref.at[:, pl.ds(pl.multiple_of(left, width), width)], sem.at[at]
            )
        )
    for copy in copies:
        copy.start()
    for copy in copies:
        copy.wait()


def join(quarters, cores, chunks):
    flat = [piece for quarter in quarters for piece in quarter]
    rows, width = flat[0].shape
    return pl.pallas_call(
        functools.partial(join_kernel, cores, chunks),
        in_specs=[pl.BlockSpec(memory_space=pltpu.VMEM)] * len(flat),
        out_specs=pl.BlockSpec(memory_space=pl.ANY),
        out_shape=jax.ShapeDtypeStruct((rows, width * len(flat)), flat[0].dtype),
        scratch_shapes=[pltpu.SemaphoreType.DMA((len(flat),))],
        compiler_params=pltpu.CompilerParams(vmem_limit_bytes=SMALL),
    )(*flat)


def body(groups, seq, queries, keys, values, segment, out_weight):
    depth, columns = out_weight.shape
    cores = 2
    quarter = columns // (groups * cores)
    width = quarter // CHUNKS
    steps = seq // 4

    def go(value, move):
        return moved(value, groups, seq, move)

    def over(step):
        def move(g, s):
            to = step(s)
            return (g, to) if 0 <= to < seq else None

        return move

    on_chip = over(lambda s: s ^ 1)
    on_y = over(lambda s: s ^ 2)
    on_ring = over(lambda s: (s + 4) % seq)

    def on_x(g, s):
        return ((g + 1) % groups, s)

    def on_x_other(g, s):
        return ((g + 1) % groups, s ^ 1)

    packed, own_segment, own, give = prepare(keys, values, segment, out_weight, cores, quarter)
    got = go(give, on_chip)
    back2 = go(packed, over(lambda s: s + 2))
    back_odd = go(packed, over(lambda s: s + 1 if s % 2 == 0 else s + 3))
    back_swap = go(back2, on_chip)
    mine = paired(own, got)
    line = [mine]
    across = []
    across.append([go(mine, on_y)])
    for step in range(1, steps):
        line.append(go(line[-1], on_ring))
        if step < steps - 1:
            across.append([go(line[-1], on_y)])
        else:
            last = []
            for chunk in range(CHUNKS):
                last.append(go(line[-1][:, chunk * width : (chunk + 1) * width], on_y))
            across.append(last)
    windows = (packed, back2, back_odd, back_swap)
    near, near_other, far, far_other = [], [], [], []
    for part in range(ATT_PARTS):
        near.append(attend(queries, own_segment, windows, part, ATT_PARTS))
        far.append(go(near[part], on_x))
        near_other.append(go(near[part], on_chip))
        far_other.append(go(far[part], on_chip))
    quarters = [[], [], [], []]
    for chunk in range(CHUNKS):
        pieces, layout = [], []
        for step in range(steps):
            pieces.append(line[step])
            layout.append((0, step, chunk * width))
            whole = step < steps - 1
            pieces.append(across[step][0 if whole else chunk])
            layout.append((1, step, chunk * width if whole else 0))
        same, other = project(far, far_other, pieces, tuple(layout), seq, depth, width)
        quarters[2].append(go(same, on_x))
        quarters[3].append(go(other, on_x_other))
        same, other = project(near, near_other, pieces, tuple(layout), seq, depth, width)
        quarters[0].append(same)
        quarters[1].append(go(other, on_chip))
    return join(quarters, cores, CHUNKS)


def solution(mesh):
    in_specs = (
        P(("groups", "seq"), None),
        P(("groups", "seq"), None),
        P(("groups", "seq"), None),
        P(("groups", "seq")),
        P("seq", None),
    )
    out_specs = P(("groups", "seq"), None)
    local = functools.partial(body, mesh.shape["groups"], mesh.shape["seq"])
    return jax.shard_map(local, mesh=mesh, in_specs=in_specs, out_specs=out_specs, check_vma=False)
```

```python
import functools
import math

import jax
import jax.numpy as jnp
from jax import lax
from jax.experimental import pallas as pl
from jax.experimental.pallas import tpu as pltpu
from jax.sharding import PartitionSpec as P


HEADS = 16
KV_HEADS = 4
HEAD = 128
SPAN = 4
GROUP = HEADS // KV_HEADS
EXTRA = 16
SHARES = (4, 4)
SPLITS = (1, 2)
CHUNKS = len(SHARES)
PARTS = [(c, p) for c in range(CHUNKS) for p in range(SPLITS[c])]
ATT_PARTS = 2
BELOW = -1e30
SMALL = 12 << 20
AXES = ("groups", "seq")


def moved(value, groups, seq, move):
    route = []
    for g in range(groups):
        for s in range(seq):
            to = move(g, s)
            if to is not None:
                route.append((g * seq + s, to[0] * seq + to[1]))
    return lax.ppermute(value, AXES, route)


def attention_kernel(q_ref, sq_ref, *refs):
    count = SPAN
    k_refs, v_refs, s_refs = refs[:count], refs[count : 2 * count], refs[2 * count : 3 * count]
    o_ref, bias_ref = refs[3 * count], refs[3 * count + 1]
    rows = q_ref.shape[0]
    me = lax.axis_index("seq")
    odd = lax.rem(me, 2)
    sources = (me, me - 2, me - 3 + 2 * odd, me - 1 - 2 * odd)

    @pl.when(pl.program_id(0) == 0)
    def _():
        own = sq_ref[:, 0:1].astype(jnp.float32)
        for block in range(count):
            there = s_refs[block][0:1, :].astype(jnp.float32)
            there = jnp.where(sources[block] >= 0, there, -1.0)
            live = own == there
            if block == 0:
                at_row = lax.broadcasted_iota(jnp.int32, (rows, rows), 0)
                at_column = lax.broadcasted_iota(jnp.int32, (rows, rows), 1)
                live = live & (at_column <= at_row)
            bias_ref[:, block * rows : (block + 1) * rows] = jnp.where(live, 0.0, BELOW)

    scale = HEAD ** (-0.5) * math.log2(math.e)
    for head in range(GROUP):
        q = q_ref[:, head * HEAD : (head + 1) * HEAD]
        scores = []
        for block in range(count):
            s = lax.dot_general(
                q, k_refs[block][0:rows, :], (((1,), (1,)), ((), ())),
                preferred_element_type=jnp.float32,
            )
            scores.append(s + bias_ref[:, block * rows : (block + 1) * rows])
        top = functools.reduce(jnp.maximum, scores)
        top = jnp.max(top, axis=1, keepdims=True)
        total = None
        mixed = None
        for block in range(count):
            weights = jnp.exp2((scores[block] - top) * scale)
            total = weights if total is None else total + weights
            part = jnp.dot(
                weights.astype(jnp.bfloat16), v_refs[block][0:rows, :],
                preferred_element_type=jnp.float32,
            )
            mixed = part if mixed is None else mixed + part
        total = jnp.sum(total, axis=1, keepdims=True)
        o_ref[:, head * HEAD : (head + 1) * HEAD] = (mixed / total).astype(o_ref.dtype)


def attend(queries, own_segment, windows, first, parts):
    rows = queries.shape[0]
    width = GROUP * HEAD
    groups = KV_HEADS // parts
    base = first * groups
    rows_in = windows[0].shape[0]
    k_spec = pl.BlockSpec((rows_in, HEAD), lambda i: (0, base + i))
    v_spec = pl.BlockSpec((rows_in, HEAD), lambda i: (0, KV_HEADS + base + i))
    s_spec = pl.BlockSpec((EXTRA, rows), lambda i: (rows // EXTRA, 0))
    flops = 4 * rows * SPAN * rows * HEAD * GROUP * groups
    return pl.pallas_call(
        attention_kernel,
        grid=(groups,),
        in_specs=[
            pl.BlockSpec((rows, width), lambda i: (0, base + i)),
            pl.BlockSpec((rows, HEAD), lambda i: (0, 0)),
        ]
        + [k_spec] * SPAN
        + [v_spec] * SPAN
        + [s_spec] * SPAN,
        out_specs=pl.BlockSpec((rows, width), lambda i: (0, i)),
        out_shape=jax.ShapeDtypeStruct((rows, groups * width), jnp.bfloat16),
        scratch_shapes=[pltpu.VMEM((rows, SPAN * rows), jnp.float32)],
        cost_estimate=pl.CostEstimate(
            flops=flops, bytes_accessed=4 * rows * groups * width, transcendentals=rows * rows * SPAN * GROUP * groups
        ),
        compiler_params=pltpu.CompilerParams(vmem_limit_bytes=SMALL),
    )(queries, own_segment, *windows, *windows, *windows)


def prep_kernel(cores, k_ref, v_ref, seg_ref, w_ref, packed_ref, col_ref, own_ref, give_ref, sem):
    rows, kept = k_ref.shape
    width = own_ref.shape[1]
    core = lax.rem(lax.axis_index("seq"), cores)
    base = lax.axis_index("groups") * cores
    mine = pl.ds(pl.multiple_of((base + core) * width, width), width)
    other = pl.ds(pl.multiple_of((base + cores - 1 - core) * width, width), width)
    copies = [
        pltpu.make_async_copy(w_ref.at[:, other], give_ref, sem.at[0]),
        pltpu.make_async_copy(k_ref, packed_ref.at[0:rows, 0:kept], sem.at[1]),
        pltpu.make_async_copy(v_ref, packed_ref.at[0:rows, kept : 2 * kept], sem.at[2]),
        pltpu.make_async_copy(w_ref.at[:, mine], own_ref, sem.at[3]),
    ]
    for copy in copies:
        copy.start()
    marks = seg_ref[...].astype(jnp.float32)
    column = jnp.transpose(jnp.broadcast_to(marks, (HEAD, rows)))
    col_ref[...] = column.astype(col_ref.dtype)
    packed_ref[rows:, :] = jnp.zeros((EXTRA, 2 * kept), packed_ref.dtype)
    packed_ref[rows:, 0:rows] = jnp.broadcast_to(marks, (EXTRA, rows)).astype(packed_ref.dtype)
    for copy in copies:
        copy.wait()


def prepare(keys, values, segment, out_weight, cores, width):
    rows, kept = keys.shape
    depth = out_weight.shape[0]
    in_hbm = pl.BlockSpec(memory_space=pltpu.HBM)
    in_vmem = pl.BlockSpec(memory_space=pltpu.VMEM)
    kind = keys.dtype
    keys, values, out_weight = [
        pltpu.with_memory_space_constraint(v, pltpu.HBM) for v in (keys, values, out_weight)
    ]
    return pl.pallas_call(
        functools.partial(prep_kernel, cores),
        in_specs=[in_hbm, in_hbm, in_vmem, in_hbm],
        out_specs=[in_vmem] * 4,
        out_shape=[
            jax.ShapeDtypeStruct((rows + EXTRA, 2 * kept), kind),
            jax.ShapeDtypeStruct((rows, HEAD), kind),
            jax.ShapeDtypeStruct((depth, width), kind),
            jax.ShapeDtypeStruct((depth, width), kind),
        ],
        scratch_shapes=[pltpu.SemaphoreType.DMA((4,))],
        compiler_params=pltpu.CompilerParams(vmem_limit_bytes=SMALL),
    )(keys, values, segment[None, :], out_weight)


def pair_kernel(edges, a_ref, b_ref, *o_refs):
    depth = a_ref.shape[0]
    core = lax.rem(lax.axis_index("seq"), 2)
    for half, ref in enumerate((a_ref, b_ref)):
        top = pl.multiple_of((core if half == 0 else 1 - core) * depth, depth)
        for o_ref, left, right in zip(o_refs, edges, edges[1:]):
            o_ref[pl.ds(top, depth), :] = ref[:, left:right]
        o_refs[-1][pl.ds(top, depth), :] = ref[...]


def paired(own, got, edges):
    in_vmem = pl.BlockSpec(memory_space=pltpu.VMEM)
    depth = 2 * own.shape[0]
    widths = [right - left for left, right in zip(edges, edges[1:])] + [own.shape[1]]
    return pl.pallas_call(
        functools.partial(pair_kernel, edges),
        in_specs=[in_vmem] * 2, out_specs=[in_vmem] * len(widths),
        out_shape=[jax.ShapeDtypeStruct((depth, width), own.dtype) for width in widths],
        compiler_params=pltpu.CompilerParams(vmem_limit_bytes=SMALL),
    )(own, got)


def project_kernel(layout, depth, parts, *refs):
    att_refs = refs[: 2 * parts]
    piece_refs = refs[2 * parts : 2 * parts + len(layout)]
    o_refs = refs[2 * parts + len(layout) : 2 * parts + len(layout) + 2]
    stacked, *rest = refs[2 * parts + len(layout) + 2 :]
    width = o_refs[0].shape[1]
    rows, span = att_refs[0].shape
    chip = lax.axis_index("seq") // 2
    deep = 2 * depth
    near = lax.rem(chip, 2)
    sources = [
        2 * source(chip // 2) + (near if flip == 0 else 1 - near) for flip, source, _ in layout
    ]
    if rest:
        held, sem = rest
        for piece, (_, _, base), source in zip(piece_refs, layout, sources):
            where = pl.ds(pl.multiple_of(source * deep, deep), deep)
            pltpu.make_async_copy(piece.at[:, base : base + width], held.at[where, :], sem).start()
        pltpu.make_async_copy(held, held, sem).wait()
    for which in range(2):
        for part in range(parts):
            stacked[part, which * rows : (which + 1) * rows, :] = att_refs[which * parts + part][...]
    for left in range(0, width, 256):
        tile = min(256, width - left)
        terms = []
        if rest:
            for part in range(parts):
                terms.append((stacked[part], held[part * span : (part + 1) * span, left : left + tile]))
        else:
            for piece, (_, _, base), source in zip(piece_refs, layout, sources):
                at = source * deep
                part = at // span
                columns = pl.ds(pl.multiple_of(at - part * span, deep), deep)
                terms.append((stacked[part, :, columns], piece[:, base + left : base + left + tile]))
        total = None
        for a, w in terms:
            product = jnp.dot(a, w, preferred_element_type=jnp.float32)
            total = product if total is None else total + product
        for which in range(2):
            o_refs[which][:, left : left + tile] = total[which * rows : (which + 1) * rows].astype(
                o_refs[which].dtype
            )


def project(first, second, pieces, layout, seq, depth, width):
    parts = len(first)
    rows, span = first[0].shape
    inner = seq * depth
    in_vmem = pl.BlockSpec(memory_space=pltpu.VMEM)
    direct = (2 * depth) % HEAD == 0 and span % (2 * depth) == 0
    shape = jax.ShapeDtypeStruct((rows, width), jnp.bfloat16)
    scratch = [pltpu.VMEM((parts, 2 * rows, span), jnp.bfloat16)]
    if not direct:
        scratch += [pltpu.VMEM((inner, width), jnp.bfloat16), pltpu.SemaphoreType.DMA]
    piece_spec = in_vmem if direct else pl.BlockSpec(memory_space=pl.ANY)
    return pl.pallas_call(
        functools.partial(project_kernel, layout, depth, parts),
        in_specs=[in_vmem] * (2 * parts) + [piece_spec] * len(pieces),
        out_specs=[in_vmem] * 2,
        out_shape=[shape, shape],
        scratch_shapes=scratch,
        cost_estimate=pl.CostEstimate(
            flops=4 * rows * inner * width, bytes_accessed=2 * inner * width, transcendentals=0
        ),
        compiler_params=pltpu.CompilerParams(vmem_limit_bytes=SMALL),
    )(*first, *second, *pieces)


def join_kernel(cores, edges, *refs):
    o_ref, sem = refs[-2:]
    chunks = len(edges) - 1
    core = lax.rem(lax.axis_index("seq"), cores)
    group = lax.axis_index("groups")
    copies = []
    for at, ref in enumerate(refs[:-2]):
        quarter, chunk = at // chunks, at % chunks
        from_group = group if quarter < 2 else 1 - group
        from_core = core if quarter % 2 == 0 else 1 - core
        left = (from_group * cores + from_core) * edges[-1] + edges[chunk]
        place = pl.ds(pl.multiple_of(left, math.gcd(*edges)), ref.shape[1])
        copies.append(pltpu.make_async_copy(ref, o_ref.at[:, place], sem.at[at]))
    for copy in copies:
        copy.start()
    for copy in copies:
        copy.wait()


def join(quarters, cores, edges):
    flat = [piece for quarter in quarters for piece in quarter]
    rows = flat[0].shape[0]
    return pl.pallas_call(
        functools.partial(join_kernel, cores, edges),
        in_specs=[pl.BlockSpec(memory_space=pltpu.VMEM)] * len(flat),
        out_specs=pl.BlockSpec(memory_space=pl.ANY),
        out_shape=jax.ShapeDtypeStruct((rows, edges[-1] * len(quarters)), flat[0].dtype),
        scratch_shapes=[pltpu.SemaphoreType.DMA((len(flat),))],
        compiler_params=pltpu.CompilerParams(vmem_limit_bytes=SMALL),
    )(*flat)


def ring_plan(steps):
    ops, slots = {}, []
    for way, sign, count in (("f", 1, steps // 2), ("b", -1, (steps - 1) // 2)):
        before = None
        for step in range(1, count + 1):
            name = f"{way}{step}"
            ops[name] = (before, lambda z, c, sign=sign: ((z + sign) % steps, c))
            slots.append((name, (name,), lambda z, k=sign * step: lax.rem(z - k + 2 * steps, steps)))
            before = name
    return ops, slots


def line_plan():
    def inner(z, c):
        return (3 - z, c) if 0 < z < 3 else (z, 1 - c)

    def side(z, c):
        return (z ^ 1, c)

    ops = {
        "a": (None, side),
        "b": (None, inner),
        "c": ("a", inner),
        "d": ("b", side),
        "e": ("c", side),
    }
    slots = [
        ("a", ("a",), lambda z: lax.bitwise_xor(z, 1)),
        ("d", ("b", "d"), lambda z: 2 - z // 2),
        ("e", ("c", "e"), lambda z: 3 - 3 * (z // 2)),
    ]
    return ops, slots


def plan(steps):
    return line_plan() if steps == 4 else ring_plan(steps)


def body(groups, seq, queries, keys, values, segment, out_weight):
    depth, columns = out_weight.shape
    cores = 2
    quarter = columns // (groups * cores)
    whole = sum(SHARES)
    edges = tuple(quarter * sum(SHARES[:k]) // whole for k in range(CHUNKS + 1))
    spans = []
    for c, p in PARTS:
        size = (edges[c + 1] - edges[c]) // SPLITS[c]
        spans.append((p * size, (p + 1) * size))
    cuts = tuple(edges[c] + left for (c, _), (left, _) in zip(PARTS, spans)) + (quarter,)
    steps = seq // 4

    def go(value, move):
        return moved(value, groups, seq, move)

    def over(step):
        def move(g, s):
            to = step(s)
            return (g, to) if 0 <= to < seq else None

        return move

    on_chip = over(lambda s: s ^ 1)
    on_y = over(lambda s: s ^ 2)
    ops, slots = plan(steps)
    place = lax.axis_index("seq") // 4
    inside = (place > 0) & (place < steps - 1)

    def along(step):
        def move(g, s):
            z, c = step(s // 4, s % 2)
            return (g, 4 * z + s % 4 // 2 * 2 + c)

        return move


    def on_x(g, s):
        return ((g + 1) % groups, s)

    def on_x_other(g, s):
        return ((g + 1) % groups, s ^ 1)

    packed, own_segment, own, give = prepare(keys, values, segment, out_weight, cores, quarter)
    got = go(give, on_chip)
    back2 = go(packed, over(lambda s: (s + 2) % seq))
    back_odd = go(packed, over(lambda s: (s + 1 if s % 2 == 0 else s + 3) % seq))
    back_swap = go(back2, on_chip)
    *mine, mine_all = paired(own, got, edges)
    across_all = go(mine_all, on_y)
    pieces = [[] for _ in PARTS]
    layout = [[] for _ in PARTS]

    def arrived(chunk, value, flip, shift, left=0, only=None):
        for at, (c, _) in enumerate(PARTS):
            if c == chunk and only in (None, at):
                pieces[at].append(value)
                layout[at].append((flip, shift, 0 if only is not None else left + spans[at][0]))

    for chunk in range(CHUNKS):
        arrived(chunk, mine[chunk], 0, lambda z: z)
        arrived(chunk, across_all, 1, lambda z: z, edges[chunk])
        lines = {None: mine[chunk]}
        for name, (before, step) in ops.items():
            lines[name] = go(lines[before], along(step))
        for name, kinds, source in slots:
            line = lines[kinds[0]]
            if len(kinds) > 1:
                line = jnp.where(inside, line, lines[kinds[1]])
            arrived(chunk, line, 0, source)
            if name == slots[-1][0] and SPLITS[chunk] > 1:
                for at, (c, p) in enumerate(PARTS):
                    if c == chunk:
                        across = go(line[:, spans[at][0] : spans[at][1]], on_y)
                        arrived(chunk, across, 1, source, only=at)
            else:
                across = go(line, on_y)
                arrived(chunk, across, 1, source)
    windows = (packed, back2, back_odd, back_swap)
    near, near_other, far, far_other = [], [], [], []
    for part in range(ATT_PARTS):
        near.append(attend(queries, own_segment, windows, part, ATT_PARTS))
        far.append(go(near[part], on_x))
        near_other.append(go(near[part], on_chip))
        far_other.append(go(far[part], on_chip))
    quarters = [[], [], [], []]
    for at in range(len(PARTS)):
        args = (pieces[at], tuple(layout[at]), seq, depth, spans[at][1] - spans[at][0])
        same, other = project(far, far_other, *args)
        quarters[2].append(go(same, on_x))
        quarters[3].append(go(other, on_x_other))
        same, other = project(near, near_other, *args)
        quarters[0].append(same)
        quarters[1].append(go(other, on_chip))
    return join(quarters, cores, cuts)


def solution(mesh):
    in_specs = (
        P(("groups", "seq"), None),
        P(("groups", "seq"), None),
        P(("groups", "seq"), None),
        P(("groups", "seq")),
        P("seq", None),
    )
    out_specs = P(("groups", "seq"), None)
    local = functools.partial(body, mesh.shape["groups"], mesh.shape["seq"])
    return jax.shard_map(local, mesh=mesh, in_specs=in_specs, out_specs=out_specs, check_vma=False)
```

```python
import functools
import math

import jax
import jax.numpy as jnp
from jax import lax
from jax.experimental import pallas as pl
from jax.experimental.pallas import tpu as pltpu
from jax.sharding import PartitionSpec as P


HEADS = 16
KV_HEADS = 4
HEAD = 128
SPAN = 4
GROUP = HEADS // KV_HEADS
EXTRA = 16
SHARES = (4, 4)
SPLITS = (1, 2)
CHUNKS = len(SHARES)
PARTS = [(c, p) for c in range(CHUNKS) for p in range(SPLITS[c])]
ATT_PARTS = 2
BELOW = -1e30
SMALL = 12 << 20
AXES = ("groups", "seq")


def moved(value, groups, seq, move):
    route = []
    for g in range(groups):
        for s in range(seq):
            to = move(g, s)
            if to is not None:
                route.append((g * seq + s, to[0] * seq + to[1]))
    return lax.ppermute(value, AXES, route)


def attention_kernel(q_ref, sq_ref, *refs):
    count = SPAN
    k_refs, v_refs, s_refs = refs[:count], refs[count : 2 * count], refs[2 * count : 3 * count]
    o_ref, bias_ref = refs[3 * count], refs[3 * count + 1]
    rows = q_ref.shape[0]
    me = lax.axis_index("seq")
    odd = lax.rem(me, 2)
    sources = (me, me - 2, me - 3 + 2 * odd, me - 1 - 2 * odd)

    @pl.when(pl.program_id(0) == 0)
    def _():
        own = sq_ref[:, 0:1].astype(jnp.float32)
        for block in range(count):
            there = s_refs[block][0:1, :].astype(jnp.float32)
            there = jnp.where(sources[block] >= 0, there, -1.0)
            live = own == there
            if block == 0:
                at_row = lax.broadcasted_iota(jnp.int32, (rows, rows), 0)
                at_column = lax.broadcasted_iota(jnp.int32, (rows, rows), 1)
                live = live & (at_column <= at_row)
            bias_ref[:, block * rows : (block + 1) * rows] = jnp.where(live, 0.0, BELOW)

    scale = HEAD ** (-0.5) * math.log2(math.e)
    for head in range(GROUP):
        q = q_ref[:, head * HEAD : (head + 1) * HEAD]
        scores = []
        for block in range(count):
            s = lax.dot_general(
                q, k_refs[block][0:rows, :], (((1,), (1,)), ((), ())),
                preferred_element_type=jnp.float32,
            )
            scores.append(s + bias_ref[:, block * rows : (block + 1) * rows])
        top = functools.reduce(jnp.maximum, scores)
        top = jnp.max(top, axis=1, keepdims=True)
        total = None
        mixed = None
        for block in range(count):
            weights = jnp.exp2((scores[block] - top) * scale)
            total = weights if total is None else total + weights
            part = jnp.dot(
                weights.astype(jnp.bfloat16), v_refs[block][0:rows, :],
                preferred_element_type=jnp.float32,
            )
            mixed = part if mixed is None else mixed + part
        total = jnp.sum(total, axis=1, keepdims=True)
        o_ref[:, head * HEAD : (head + 1) * HEAD] = (mixed / total).astype(o_ref.dtype)


def attend(queries, own_segment, windows, first, parts):
    rows = queries.shape[0]
    width = GROUP * HEAD
    groups = KV_HEADS // parts
    base = first * groups
    rows_in = windows[0].shape[0]
    k_spec = pl.BlockSpec((rows_in, HEAD), lambda i: (0, base + i))
    v_spec = pl.BlockSpec((rows_in, HEAD), lambda i: (0, KV_HEADS + base + i))
    s_spec = pl.BlockSpec((EXTRA, rows), lambda i: (rows // EXTRA, 0))
    flops = 4 * rows * SPAN * rows * HEAD * GROUP * groups
    return pl.pallas_call(
        attention_kernel,
        grid=(groups,),
        in_specs=[
            pl.BlockSpec((rows, width), lambda i: (0, base + i)),
            pl.BlockSpec((rows, HEAD), lambda i: (0, 0)),
        ]
        + [k_spec] * SPAN
        + [v_spec] * SPAN
        + [s_spec] * SPAN,
        out_specs=pl.BlockSpec((rows, width), lambda i: (0, i)),
        out_shape=jax.ShapeDtypeStruct((rows, groups * width), jnp.bfloat16),
        scratch_shapes=[pltpu.VMEM((rows, SPAN * rows), jnp.float32)],
        cost_estimate=pl.CostEstimate(
            flops=flops, bytes_accessed=4 * rows * groups * width, transcendentals=rows * rows * SPAN * GROUP * groups
        ),
        compiler_params=pltpu.CompilerParams(vmem_limit_bytes=SMALL),
    )(queries, own_segment, *windows, *windows, *windows)


def prep_kernel(
    cores, k_ref, v_ref, seg_ref, w_ref, packed_ref, col_ref, own_ref, give_ref, seg, sem
):
    rows, kept = k_ref.shape
    width = own_ref.shape[1]
    core = lax.rem(lax.axis_index("seq"), cores)
    base = lax.axis_index("groups") * cores
    mine = pl.ds(pl.multiple_of((base + core) * width, width), width)
    other = pl.ds(pl.multiple_of((base + cores - 1 - core) * width, width), width)
    copies = [
        pltpu.make_async_copy(seg_ref, seg, sem.at[4]),
        pltpu.make_async_copy(w_ref.at[:, other], give_ref, sem.at[0]),
        pltpu.make_async_copy(k_ref, packed_ref.at[0:rows, 0:kept], sem.at[1]),
        pltpu.make_async_copy(v_ref, packed_ref.at[0:rows, kept : 2 * kept], sem.at[2]),
        pltpu.make_async_copy(w_ref.at[:, mine], own_ref, sem.at[3]),
    ]
    for copy in copies:
        copy.start()
    copies[0].wait()
    marks = seg[...].astype(jnp.float32)
    column = jnp.transpose(jnp.broadcast_to(marks, (HEAD, rows)))
    col_ref[...] = column.astype(col_ref.dtype)
    packed_ref[rows:, :] = jnp.zeros((EXTRA, 2 * kept), packed_ref.dtype)
    packed_ref[rows:, 0:rows] = jnp.broadcast_to(marks, (EXTRA, rows)).astype(packed_ref.dtype)
    for copy in copies[1:]:
        copy.wait()


def prepare(keys, values, segment, out_weight, cores, width):
    rows, kept = keys.shape
    depth = out_weight.shape[0]
    in_hbm = pl.BlockSpec(memory_space=pltpu.HBM)
    in_vmem = pl.BlockSpec(memory_space=pltpu.VMEM)
    kind = keys.dtype
    given = (keys, values, segment[None, :], out_weight)
    given = [pltpu.with_memory_space_constraint(v, pltpu.HBM) for v in given]
    return pl.pallas_call(
        functools.partial(prep_kernel, cores),
        in_specs=[in_hbm] * 4,
        out_specs=[in_vmem] * 4,
        out_shape=[
            jax.ShapeDtypeStruct((rows + EXTRA, 2 * kept), kind),
            jax.ShapeDtypeStruct((rows, HEAD), kind),
            jax.ShapeDtypeStruct((depth, width), kind),
            jax.ShapeDtypeStruct((depth, width), kind),
        ],
        scratch_shapes=[pltpu.VMEM((1, rows), jnp.int32), pltpu.SemaphoreType.DMA((5,))],
        compiler_params=pltpu.CompilerParams(vmem_limit_bytes=SMALL),
    )(*given)


def pair_kernel(edges, a_ref, b_ref, *o_refs):
    depth = a_ref.shape[0]
    core = lax.rem(lax.axis_index("seq"), 2)
    for half, ref in enumerate((a_ref, b_ref)):
        top = pl.multiple_of((core if half == 0 else 1 - core) * depth, depth)
        for o_ref, left, right in zip(o_refs, edges, edges[1:]):
            o_ref[pl.ds(top, depth), :] = ref[:, left:right]
        o_refs[-1][pl.ds(top, depth), :] = ref[...]


def paired(own, got, edges):
    in_vmem = pl.BlockSpec(memory_space=pltpu.VMEM)
    depth = 2 * own.shape[0]
    widths = [right - left for left, right in zip(edges, edges[1:])] + [own.shape[1]]
    return pl.pallas_call(
        functools.partial(pair_kernel, edges),
        in_specs=[in_vmem] * 2, out_specs=[in_vmem] * len(widths),
        out_shape=[jax.ShapeDtypeStruct((depth, width), own.dtype) for width in widths],
        compiler_params=pltpu.CompilerParams(vmem_limit_bytes=SMALL),
    )(own, got)


def project_kernel(layout, depth, parts, *refs):
    att_refs = refs[: 2 * parts]
    piece_refs = refs[2 * parts : 2 * parts + len(layout)]
    o_refs = refs[2 * parts + len(layout) : 2 * parts + len(layout) + 2]
    stacked, *rest = refs[2 * parts + len(layout) + 2 :]
    width = o_refs[0].shape[1]
    rows, span = att_refs[0].shape
    chip = lax.axis_index("seq") // 2
    deep = 2 * depth
    near = lax.rem(chip, 2)
    sources = [
        2 * source(chip // 2) + (near if flip == 0 else 1 - near) for flip, source, _ in layout
    ]
    if rest:
        held, sem = rest
        for piece, (_, _, base), source in zip(piece_refs, layout, sources):
            where = pl.ds(pl.multiple_of(source * deep, deep), deep)
            pltpu.make_async_copy(piece.at[:, base : base + width], held.at[where, :], sem).start()
        pltpu.make_async_copy(held, held, sem).wait()
    for which in range(2):
        for part in range(parts):
            stacked[part, which * rows : (which + 1) * rows, :] = att_refs[which * parts + part][...]
    for left in range(0, width, 256):
        tile = min(256, width - left)
        terms = []
        if rest:
            for part in range(parts):
                terms.append((stacked[part], held[part * span : (part + 1) * span, left : left + tile]))
        else:
            for piece, (_, _, base), source in zip(piece_refs, layout, sources):
                at = source * deep
                part = at // span
                columns = pl.ds(pl.multiple_of(at - part * span, deep), deep)
                terms.append((stacked[part, :, columns], piece[:, base + left : base + left + tile]))
        total = None
        for a, w in terms:
            product = jnp.dot(a, w, preferred_element_type=jnp.float32)
            total = product if total is None else total + product
        for which in range(2):
            o_refs[which][:, left : left + tile] = total[which * rows : (which + 1) * rows].astype(
                o_refs[which].dtype
            )


def project(first, second, pieces, layout, seq, depth, width):
    parts = len(first)
    rows, span = first[0].shape
    inner = seq * depth
    in_vmem = pl.BlockSpec(memory_space=pltpu.VMEM)
    direct = (2 * depth) % HEAD == 0 and span % (2 * depth) == 0
    shape = jax.ShapeDtypeStruct((rows, width), jnp.bfloat16)
    scratch = [pltpu.VMEM((parts, 2 * rows, span), jnp.bfloat16)]
    if not direct:
        scratch += [pltpu.VMEM((inner, width), jnp.bfloat16), pltpu.SemaphoreType.DMA]
    piece_spec = in_vmem if direct else pl.BlockSpec(memory_space=pl.ANY)
    return pl.pallas_call(
        functools.partial(project_kernel, layout, depth, parts),
        in_specs=[in_vmem] * (2 * parts) + [piece_spec] * len(pieces),
        out_specs=[in_vmem] * 2,
        out_shape=[shape, shape],
        scratch_shapes=scratch,
        cost_estimate=pl.CostEstimate(
            flops=4 * rows * inner * width, bytes_accessed=2 * inner * width, transcendentals=0
        ),
        compiler_params=pltpu.CompilerParams(vmem_limit_bytes=SMALL),
    )(*first, *second, *pieces)


def join_kernel(cores, places, *refs):
    pieces = refs[: len(places)]
    o_ref, sem = refs[-2:]
    core = lax.rem(lax.axis_index("seq"), cores)
    group = lax.axis_index("groups")
    copies = []
    for at, (ref, (quarter, width, cut)) in enumerate(zip(pieces, places)):
        from_group = group if quarter < 2 else 1 - group
        from_core = core if quarter % 2 == 0 else 1 - core
        left = (from_group * cores + from_core) * width + cut
        place = pl.ds(pl.multiple_of(left, math.gcd(width, cut, HEAD)), ref.shape[1])
        copies.append(pltpu.make_async_copy(ref, o_ref.at[:, place], sem.at[at]))
    for copy in copies:
        copy.start()
    for copy in copies:
        copy.wait()


def join(pieces, places, cores, columns, before=None):
    in_hbm = pl.BlockSpec(memory_space=pl.ANY)
    earlier = [] if before is None else [before]
    return pl.pallas_call(
        functools.partial(join_kernel, cores, tuple(places)),
        in_specs=[pl.BlockSpec(memory_space=pltpu.VMEM)] * len(pieces) + [in_hbm] * len(earlier),
        out_specs=in_hbm,
        out_shape=jax.ShapeDtypeStruct((pieces[0].shape[0], columns), pieces[0].dtype),
        input_output_aliases={len(pieces): 0} if earlier else {},
        scratch_shapes=[pltpu.SemaphoreType.DMA((len(pieces),))],
        compiler_params=pltpu.CompilerParams(vmem_limit_bytes=SMALL),
    )(*pieces, *earlier)


def ring_plan(steps):
    ops, slots = {}, []
    for way, sign, count in (("f", 1, steps // 2), ("b", -1, (steps - 1) // 2)):
        before = None
        for step in range(1, count + 1):
            name = f"{way}{step}"
            ops[name] = (before, lambda z, c, sign=sign: ((z + sign) % steps, c))
            slots.append((name, (name,), lambda z, k=sign * step: lax.rem(z - k + 2 * steps, steps)))
            before = name
    return ops, slots


def line_plan():
    def inner(z, c):
        return (3 - z, c) if 0 < z < 3 else (z, 1 - c)

    def side(z, c):
        return (z ^ 1, c)

    ops = {
        "a": (None, side),
        "b": (None, inner),
        "c": ("a", inner),
        "d": ("b", side),
        "e": ("c", side),
    }
    slots = [
        ("a", ("a",), lambda z: lax.bitwise_xor(z, 1)),
        ("d", ("b", "d"), lambda z: 2 - z // 2),
        ("e", ("c", "e"), lambda z: 3 - 3 * (z // 2)),
    ]
    return ops, slots


def plan(steps):
    return line_plan() if steps == 4 else ring_plan(steps)


def body(groups, seq, queries, keys, values, segment, out_weight):
    depth, columns = out_weight.shape
    cores = 2
    quarter = columns // (groups * cores)
    whole = sum(SHARES)
    edges = tuple(quarter * sum(SHARES[:k]) // whole for k in range(CHUNKS + 1))
    spans = []
    for c, p in PARTS:
        size = (edges[c + 1] - edges[c]) // SPLITS[c]
        spans.append((p * size, (p + 1) * size))
    cuts = tuple(edges[c] + left for (c, _), (left, _) in zip(PARTS, spans)) + (quarter,)
    steps = seq // 4

    def go(value, move):
        return moved(value, groups, seq, move)

    def over(step):
        def move(g, s):
            to = step(s)
            return (g, to) if 0 <= to < seq else None

        return move

    on_chip = over(lambda s: s ^ 1)
    on_y = over(lambda s: s ^ 2)
    ops, slots = plan(steps)
    place = lax.axis_index("seq") // 4
    inside = (place > 0) & (place < steps - 1)

    def along(step):
        def move(g, s):
            z, c = step(s // 4, s % 2)
            return (g, 4 * z + s % 4 // 2 * 2 + c)

        return move


    def on_x(g, s):
        return ((g + 1) % groups, s)

    def on_x_other(g, s):
        return ((g + 1) % groups, s ^ 1)

    packed, own_segment, own, give = prepare(keys, values, segment, out_weight, cores, quarter)
    got = go(give, on_chip)
    back2 = go(packed, over(lambda s: (s + 2) % seq))
    back_odd = go(packed, over(lambda s: (s + 1 if s % 2 == 0 else s + 3) % seq))
    back_swap = go(back2, on_chip)
    *mine, mine_all = paired(own, got, edges)
    across_all = go(mine_all, on_y)
    pieces = [[] for _ in PARTS]
    layout = [[] for _ in PARTS]

    def arrived(chunk, value, flip, shift, left=0, only=None):
        for at, (c, _) in enumerate(PARTS):
            if c == chunk and only in (None, at):
                pieces[at].append(value)
                layout[at].append((flip, shift, 0 if only is not None else left + spans[at][0]))

    for chunk in range(CHUNKS):
        arrived(chunk, mine[chunk], 0, lambda z: z)
        arrived(chunk, across_all, 1, lambda z: z, edges[chunk])
        lines = {None: mine[chunk]}
        for name, (before, step) in ops.items():
            lines[name] = go(lines[before], along(step))
        for name, kinds, source in slots:
            line = lines[kinds[0]]
            if len(kinds) > 1:
                line = jnp.where(inside, line, lines[kinds[1]])
            arrived(chunk, line, 0, source)
            if name == slots[-1][0] and SPLITS[chunk] > 1:
                for at, (c, p) in enumerate(PARTS):
                    if c == chunk:
                        across = go(line[:, spans[at][0] : spans[at][1]], on_y)
                        arrived(chunk, across, 1, source, only=at)
            else:
                across = go(line, on_y)
                arrived(chunk, across, 1, source)
    windows = (packed, back2, back_odd, back_swap)
    near, near_other, far, far_other = [], [], [], []
    for part in range(ATT_PARTS):
        near.append(attend(queries, own_segment, windows, part, ATT_PARTS))
        far.append(go(near[part], on_x))
        near_other.append(go(near[part], on_chip))
        far_other.append(go(far[part], on_chip))
    quarters = [[], [], [], []]
    for at in range(len(PARTS)):
        args = (pieces[at], tuple(layout[at]), seq, depth, spans[at][1] - spans[at][0])
        same, other = project(far, far_other, *args)
        quarters[2].append(go(same, on_x))
        quarters[3].append(go(other, on_x_other))
        same, other = project(near, near_other, *args)
        quarters[0].append(same)
        quarters[1].append(go(other, on_chip))
    early, late = [], []
    for at in range(len(PARTS)):
        for q in range(4):
            entry = (quarters[q][at], (q, quarter, cuts[at]))
            (late if q > 1 and at == len(PARTS) - 1 else early).append(entry)
    joined = join(*zip(*early), cores, columns)
    return join(*zip(*late), cores, columns, joined)


def solution(mesh):
    in_specs = (
        P(("groups", "seq"), None),
        P(("groups", "seq"), None),
        P(("groups", "seq"), None),
        P(("groups", "seq")),
        P("seq", None),
    )
    out_specs = P(("groups", "seq"), None)
    local = functools.partial(body, mesh.shape["groups"], mesh.shape["seq"])
    return jax.shard_map(local, mesh=mesh, in_specs=in_specs, out_specs=out_specs, check_vma=False)
```

```python
import functools
import math

import jax
import jax.numpy as jnp
from jax import lax
from jax.experimental import pallas as pl
from jax.experimental.pallas import tpu as pltpu
from jax.sharding import PartitionSpec as P


HEADS = 16
KV_HEADS = 4
HEAD = 128
SPAN = 4
GROUP = HEADS // KV_HEADS
EXTRA = 16
SHARES = (4, 4)
SPLITS = (1, 2)
CHUNKS = len(SHARES)
PARTS = [(c, p) for c in range(CHUNKS) for p in range(SPLITS[c])]
ATT_PARTS = 2
BELOW = -1e30
SMALL = 12 << 20
AXES = ("groups", "seq")


def moved(value, groups, seq, move):
    route = []
    for g in range(groups):
        for s in range(seq):
            to = move(g, s)
            if to is not None:
                route.append((g * seq + s, to[0] * seq + to[1]))
    return lax.ppermute(value, AXES, route)


def attention_kernel(q_ref, sq_ref, *refs):
    count = SPAN
    k_refs, v_refs, s_refs = refs[:count], refs[count : 2 * count], refs[2 * count : 3 * count]
    o_ref, bias_ref = refs[3 * count], refs[3 * count + 1]
    rows = q_ref.shape[0]
    me = lax.axis_index("seq")
    odd = lax.rem(me, 2)
    sources = (me, me - 2, me - 3 + 2 * odd, me - 1 - 2 * odd)

    @pl.when(pl.program_id(0) == 0)
    def _():
        own = sq_ref[:, 0:1].astype(jnp.float32)
        for block in range(count):
            there = s_refs[block][0:1, :].astype(jnp.float32)
            there = jnp.where(sources[block] >= 0, there, -1.0)
            live = own == there
            if block == 0:
                at_row = lax.broadcasted_iota(jnp.int32, (rows, rows), 0)
                at_column = lax.broadcasted_iota(jnp.int32, (rows, rows), 1)
                live = live & (at_column <= at_row)
            bias_ref[:, block * rows : (block + 1) * rows] = jnp.where(live, 0.0, BELOW)

    scale = HEAD ** (-0.5) * math.log2(math.e)
    for head in range(GROUP):
        q = q_ref[:, head * HEAD : (head + 1) * HEAD]
        scores = []
        for block in range(count):
            s = lax.dot_general(
                q, k_refs[block][0:rows, :], (((1,), (1,)), ((), ())),
                preferred_element_type=jnp.float32,
            )
            scores.append(s + bias_ref[:, block * rows : (block + 1) * rows])
        top = functools.reduce(jnp.maximum, scores)
        top = jnp.max(top, axis=1, keepdims=True)
        total = None
        mixed = None
        for block in range(count):
            weights = jnp.exp2((scores[block] - top) * scale)
            total = weights if total is None else total + weights
            part = jnp.dot(
                weights.astype(jnp.bfloat16), v_refs[block][0:rows, :],
                preferred_element_type=jnp.float32,
            )
            mixed = part if mixed is None else mixed + part
        total = jnp.sum(total, axis=1, keepdims=True)
        o_ref[:, head * HEAD : (head + 1) * HEAD] = (mixed / total).astype(o_ref.dtype)


def attend(queries, own_segment, windows, first, parts):
    rows = queries.shape[0]
    width = GROUP * HEAD
    groups = KV_HEADS // parts
    base = first * groups
    rows_in = windows[0].shape[0]
    k_spec = pl.BlockSpec((rows_in, HEAD), lambda i: (0, base + i))
    v_spec = pl.BlockSpec((rows_in, HEAD), lambda i: (0, KV_HEADS + base + i))
    s_spec = pl.BlockSpec((EXTRA, rows), lambda i: (rows // EXTRA, 0))
    flops = 4 * rows * SPAN * rows * HEAD * GROUP * groups
    return pl.pallas_call(
        attention_kernel,
        grid=(groups,),
        in_specs=[
            pl.BlockSpec((rows, width), lambda i: (0, base + i)),
            pl.BlockSpec((rows, HEAD), lambda i: (0, 0)),
        ]
        + [k_spec] * SPAN
        + [v_spec] * SPAN
        + [s_spec] * SPAN,
        out_specs=pl.BlockSpec((rows, width), lambda i: (0, i)),
        out_shape=jax.ShapeDtypeStruct((rows, groups * width), jnp.bfloat16),
        scratch_shapes=[pltpu.VMEM((rows, SPAN * rows), jnp.float32)],
        cost_estimate=pl.CostEstimate(
            flops=flops, bytes_accessed=4 * rows * groups * width, transcendentals=rows * rows * SPAN * GROUP * groups
        ),
        compiler_params=pltpu.CompilerParams(vmem_limit_bytes=SMALL),
    )(queries, own_segment, *windows, *windows, *windows)


def prep_kernel(
    cores, k_ref, v_ref, seg_ref, w_ref, packed_ref, col_ref, own_ref, give_ref, seg, sem
):
    rows, kept = k_ref.shape
    width = own_ref.shape[1]
    core = lax.rem(lax.axis_index("seq"), cores)
    base = lax.axis_index("groups") * cores
    mine = pl.ds(pl.multiple_of((base + core) * width, width), width)
    other = pl.ds(pl.multiple_of((base + cores - 1 - core) * width, width), width)
    copies = [
        pltpu.make_async_copy(seg_ref, seg, sem.at[4]),
        pltpu.make_async_copy(w_ref.at[:, other], give_ref, sem.at[0]),
        pltpu.make_async_copy(k_ref, packed_ref.at[0:rows, 0:kept], sem.at[1]),
        pltpu.make_async_copy(v_ref, packed_ref.at[0:rows, kept : 2 * kept], sem.at[2]),
        pltpu.make_async_copy(w_ref.at[:, mine], own_ref, sem.at[3]),
    ]
    for copy in copies:
        copy.start()
    copies[0].wait()
    marks = seg[...].astype(jnp.float32)
    column = jnp.transpose(jnp.broadcast_to(marks, (HEAD, rows)))
    col_ref[...] = column.astype(col_ref.dtype)
    packed_ref[rows:, :] = jnp.zeros((EXTRA, 2 * kept), packed_ref.dtype)
    packed_ref[rows:, 0:rows] = jnp.broadcast_to(marks, (EXTRA, rows)).astype(packed_ref.dtype)
    for copy in copies[1:]:
        copy.wait()


def prepare(keys, values, segment, out_weight, cores, width):
    rows, kept = keys.shape
    depth = out_weight.shape[0]
    in_hbm = pl.BlockSpec(memory_space=pltpu.HBM)
    in_vmem = pl.BlockSpec(memory_space=pltpu.VMEM)
    kind = keys.dtype
    given = (keys, values, segment[None, :], out_weight)
    given = [pltpu.with_memory_space_constraint(v, pltpu.HBM) for v in given]
    return pl.pallas_call(
        functools.partial(prep_kernel, cores),
        in_specs=[in_hbm] * 4,
        out_specs=[in_vmem] * 4,
        out_shape=[
            jax.ShapeDtypeStruct((rows + EXTRA, 2 * kept), kind),
            jax.ShapeDtypeStruct((rows, HEAD), kind),
            jax.ShapeDtypeStruct((depth, width), kind),
            jax.ShapeDtypeStruct((depth, width), kind),
        ],
        scratch_shapes=[pltpu.VMEM((1, rows), jnp.int32), pltpu.SemaphoreType.DMA((5,))],
        compiler_params=pltpu.CompilerParams(vmem_limit_bytes=SMALL),
    )(*given)


def pair_kernel(edges, a_ref, b_ref, *o_refs):
    depth = a_ref.shape[0]
    core = lax.rem(lax.axis_index("seq"), 2)
    for half, ref in enumerate((a_ref, b_ref)):
        top = pl.multiple_of((core if half == 0 else 1 - core) * depth, depth)
        for o_ref, left, right in zip(o_refs, edges, edges[1:]):
            o_ref[pl.ds(top, depth), :] = ref[:, left:right]
        o_refs[-1][pl.ds(top, depth), :] = ref[...]


def paired(own, got, edges):
    in_vmem = pl.BlockSpec(memory_space=pltpu.VMEM)
    depth = 2 * own.shape[0]
    widths = [right - left for left, right in zip(edges, edges[1:])] + [own.shape[1]]
    return pl.pallas_call(
        functools.partial(pair_kernel, edges),
        in_specs=[in_vmem] * 2, out_specs=[in_vmem] * len(widths),
        out_shape=[jax.ShapeDtypeStruct((depth, width), own.dtype) for width in widths],
        compiler_params=pltpu.CompilerParams(vmem_limit_bytes=SMALL),
    )(own, got)


def project_kernel(layout, depth, parts, *refs):
    att_refs = refs[: 2 * parts]
    piece_refs = refs[2 * parts : 2 * parts + len(layout)]
    o_refs = refs[2 * parts + len(layout) : 2 * parts + len(layout) + 2]
    stacked, *rest = refs[2 * parts + len(layout) + 2 :]
    width = o_refs[0].shape[1]
    rows, span = att_refs[0].shape
    chip = lax.axis_index("seq") // 2
    deep = 2 * depth
    near = lax.rem(chip, 2)
    sources = [
        2 * source(chip // 2) + (near if flip == 0 else 1 - near) for flip, source, _ in layout
    ]
    if rest:
        held, sem = rest
        for piece, (_, _, base), source in zip(piece_refs, layout, sources):
            where = pl.ds(pl.multiple_of(source * deep, deep), deep)
            pltpu.make_async_copy(piece.at[:, base : base + width], held.at[where, :], sem).start()
        pltpu.make_async_copy(held, held, sem).wait()
    for which in range(2):
        for part in range(parts):
            stacked[part, which * rows : (which + 1) * rows, :] = att_refs[which * parts + part][...]
    for left in range(0, width, 256):
        tile = min(256, width - left)
        terms = []
        if rest:
            for part in range(parts):
                terms.append((stacked[part], held[part * span : (part + 1) * span, left : left + tile]))
        else:
            for piece, (_, _, base), source in zip(piece_refs, layout, sources):
                at = source * deep
                part = at // span
                columns = pl.ds(pl.multiple_of(at - part * span, deep), deep)
                terms.append((stacked[part, :, columns], piece[:, base + left : base + left + tile]))
        total = None
        for a, w in terms:
            product = jnp.dot(a, w, preferred_element_type=jnp.float32)
            total = product if total is None else total + product
        for which in range(2):
            o_refs[which][:, left : left + tile] = total[which * rows : (which + 1) * rows].astype(
                o_refs[which].dtype
            )


def project(first, second, pieces, layout, seq, depth, width):
    parts = len(first)
    rows, span = first[0].shape
    inner = seq * depth
    in_vmem = pl.BlockSpec(memory_space=pltpu.VMEM)
    direct = (2 * depth) % HEAD == 0 and span % (2 * depth) == 0
    shape = jax.ShapeDtypeStruct((rows, width), jnp.bfloat16)
    scratch = [pltpu.VMEM((parts, 2 * rows, span), jnp.bfloat16)]
    if not direct:
        scratch += [pltpu.VMEM((inner, width), jnp.bfloat16), pltpu.SemaphoreType.DMA]
    piece_spec = in_vmem if direct else pl.BlockSpec(memory_space=pl.ANY)
    return pl.pallas_call(
        functools.partial(project_kernel, layout, depth, parts),
        in_specs=[in_vmem] * (2 * parts) + [piece_spec] * len(pieces),
        out_specs=[in_vmem] * 2,
        out_shape=[shape, shape],
        scratch_shapes=scratch,
        cost_estimate=pl.CostEstimate(
            flops=4 * rows * inner * width, bytes_accessed=2 * inner * width, transcendentals=0
        ),
        compiler_params=pltpu.CompilerParams(vmem_limit_bytes=SMALL),
    )(*first, *second, *pieces)


def pick_kernel(steps, spans, a_ref, b_ref, *o_refs):
    place = lax.axis_index("seq") // 4
    inside = (place > 0) & (place < steps - 1)

    def put(ref):
        o_refs[0][...] = ref[...]
        for o_ref, (left, right) in zip(o_refs[1:], spans):
            o_ref[...] = ref[:, left:right]

    @pl.when(inside)
    def _():
        put(a_ref)

    @pl.when(jnp.logical_not(inside))
    def _():
        put(b_ref)


def pick(a, b, steps, spans):
    in_vmem = pl.BlockSpec(memory_space=pltpu.VMEM)
    widths = [a.shape[1]] + [right - left for left, right in spans]
    return pl.pallas_call(
        functools.partial(pick_kernel, steps, spans),
        in_specs=[in_vmem] * 2, out_specs=[in_vmem] * len(widths),
        out_shape=[jax.ShapeDtypeStruct((a.shape[0], width), a.dtype) for width in widths],
        compiler_params=pltpu.CompilerParams(vmem_limit_bytes=SMALL),
    )(a, b)


def join_kernel(cores, places, *refs):
    pieces = refs[: len(places)]
    o_ref, sem = refs[-2:]
    core = lax.rem(lax.axis_index("seq"), cores)
    group = lax.axis_index("groups")
    copies = []
    for at, (ref, (quarter, width, cut)) in enumerate(zip(pieces, places)):
        from_group = group if quarter < 2 else 1 - group
        from_core = core if quarter % 2 == 0 else 1 - core
        left = (from_group * cores + from_core) * width + cut
        place = pl.ds(pl.multiple_of(left, math.gcd(width, cut, HEAD)), ref.shape[1])
        copies.append(pltpu.make_async_copy(ref, o_ref.at[:, place], sem.at[at]))
    for copy in copies:
        copy.start()
    for copy in copies:
        copy.wait()


def join(pieces, places, cores, columns, before=None):
    in_hbm = pl.BlockSpec(memory_space=pl.ANY)
    earlier = [] if before is None else [before]
    return pl.pallas_call(
        functools.partial(join_kernel, cores, tuple(places)),
        in_specs=[pl.BlockSpec(memory_space=pltpu.VMEM)] * len(pieces) + [in_hbm] * len(earlier),
        out_specs=in_hbm,
        out_shape=jax.ShapeDtypeStruct((pieces[0].shape[0], columns), pieces[0].dtype),
        input_output_aliases={len(pieces): 0} if earlier else {},
        scratch_shapes=[pltpu.SemaphoreType.DMA((len(pieces),))],
        compiler_params=pltpu.CompilerParams(vmem_limit_bytes=SMALL),
    )(*pieces, *earlier)


def ring_plan(steps):
    ops, slots = {}, []
    for way, sign, count in (("f", 1, steps // 2), ("b", -1, (steps - 1) // 2)):
        before = None
        for step in range(1, count + 1):
            name = f"{way}{step}"
            ops[name] = (before, lambda z, c, sign=sign: ((z + sign) % steps, c))
            slots.append((name, (name,), lambda z, k=sign * step: lax.rem(z - k + 2 * steps, steps)))
            before = name
    return ops, slots


def line_plan():
    def inner(z, c):
        return (3 - z, c) if 0 < z < 3 else (z, 1 - c)

    def side(z, c):
        return (z ^ 1, c)

    ops = {
        "a": (None, side),
        "b": (None, inner),
        "c": ("a", inner),
        "d": ("b", side),
        "e": ("c", side),
    }
    slots = [
        ("a", ("a",), lambda z: lax.bitwise_xor(z, 1)),
        ("d", ("b", "d"), lambda z: 2 - z // 2),
        ("e", ("c", "e"), lambda z: 3 - 3 * (z // 2)),
    ]
    return ops, slots


def plan(steps):
    return line_plan() if steps == 4 else ring_plan(steps)


def body(groups, seq, queries, keys, values, segment, out_weight):
    depth, columns = out_weight.shape
    cores = 2
    quarter = columns // (groups * cores)
    whole = sum(SHARES)
    edges = tuple(quarter * sum(SHARES[:k]) // whole for k in range(CHUNKS + 1))
    spans = []
    for c, p in PARTS:
        size = (edges[c + 1] - edges[c]) // SPLITS[c]
        spans.append((p * size, (p + 1) * size))
    cuts = tuple(edges[c] + left for (c, _), (left, _) in zip(PARTS, spans)) + (quarter,)
    steps = seq // 4

    def go(value, move):
        return moved(value, groups, seq, move)

    def over(step):
        def move(g, s):
            to = step(s)
            return (g, to) if 0 <= to < seq else None

        return move

    on_chip = over(lambda s: s ^ 1)
    on_y = over(lambda s: s ^ 2)
    ops, slots = plan(steps)

    def along(step):
        def move(g, s):
            z, c = step(s // 4, s % 2)
            return (g, 4 * z + s % 4 // 2 * 2 + c)

        return move


    def on_x(g, s):
        return ((g + 1) % groups, s)

    def on_x_other(g, s):
        return ((g + 1) % groups, s ^ 1)

    packed, own_segment, own, give = prepare(keys, values, segment, out_weight, cores, quarter)
    got = go(give, on_chip)
    back2 = go(packed, over(lambda s: (s + 2) % seq))
    back_odd = go(packed, over(lambda s: (s + 1 if s % 2 == 0 else s + 3) % seq))
    back_swap = go(back2, on_chip)
    *mine, mine_all = paired(own, got, edges)
    across_all = go(mine_all, on_y)
    pieces = [[] for _ in PARTS]
    layout = [[] for _ in PARTS]

    def arrived(chunk, value, flip, shift, left=0, only=None):
        for at, (c, _) in enumerate(PARTS):
            if c == chunk and only in (None, at):
                pieces[at].append(value)
                layout[at].append((flip, shift, 0 if only is not None else left + spans[at][0]))

    for chunk in range(CHUNKS):
        arrived(chunk, mine[chunk], 0, lambda z: z)
        arrived(chunk, across_all, 1, lambda z: z, edges[chunk])
        lines = {None: mine[chunk]}
        for name, (before, step) in ops.items():
            lines[name] = go(lines[before], along(step))
        for name, kinds, source in slots:
            split = name == slots[-1][0] and SPLITS[chunk] > 1
            mine_spans = [s for s, (c, _) in zip(spans, PARTS) if c == chunk] if split else []
            line = lines[kinds[0]]
            if len(kinds) > 1:
                line, *cut_lines = pick(line, lines[kinds[1]], steps, mine_spans)
            else:
                cut_lines = [line[:, left:right] for left, right in mine_spans]
            arrived(chunk, line, 0, source)
            if split:
                for at, (c, p) in enumerate(PARTS):
                    if c == chunk:
                        across = go(cut_lines[p], on_y)
                        arrived(chunk, across, 1, source, only=at)
            else:
                across = go(line, on_y)
                arrived(chunk, across, 1, source)
    windows = (packed, back2, back_odd, back_swap)
    near, near_other, far, far_other = [], [], [], []
    for part in range(ATT_PARTS):
        near.append(attend(queries, own_segment, windows, part, ATT_PARTS))
        far.append(go(near[part], on_x))
        near_other.append(go(near[part], on_chip))
        far_other.append(go(far[part], on_chip))
    quarters = [[], [], [], []]
    for at in range(len(PARTS)):
        args = (pieces[at], tuple(layout[at]), seq, depth, spans[at][1] - spans[at][0])
        same, other = project(far, far_other, *args)
        quarters[2].append(go(same, on_x))
        quarters[3].append(go(other, on_x_other))
        same, other = project(near, near_other, *args)
        quarters[0].append(same)
        quarters[1].append(go(other, on_chip))
    early, late = [], []
    for at in range(len(PARTS)):
        for q in range(4):
            entry = (quarters[q][at], (q, quarter, cuts[at]))
            (late if q > 1 and at == len(PARTS) - 1 else early).append(entry)
    joined = join(*zip(*early), cores, columns)
    return join(*zip(*late), cores, columns, joined)


def solution(mesh):
    in_specs = (
        P(("groups", "seq"), None),
        P(("groups", "seq"), None),
        P(("groups", "seq"), None),
        P(("groups", "seq")),
        P("seq", None),
    )
    out_specs = P(("groups", "seq"), None)
    local = functools.partial(body, mesh.shape["groups"], mesh.shape["seq"])
    return jax.shard_map(local, mesh=mesh, in_specs=in_specs, out_specs=out_specs, check_vma=False)
```
